256 devices in a mesh: seq: 8 (over y_lo, x), chan: 32 (over z, y_hi, core).
Axes of the slice: x: 4, y: 4 (y_hi: 2, y_lo: 2; y = y_hi * 2 + y_lo), z: 8, core: 2. Of those that a mesh axis runs over, the one named last changes fastest.
Arguments:
- post_gate: bfloat16 [2048, 8192], P('chan', 'seq'), may hold values from -6 to 6
- pre_gate: bfloat16 [2048, 8192], P('chan', 'seq'), may hold values from -6 to 6
- signal: bfloat16 [2048, 8192], P('chan', 'seq'), may hold values from -6 to 6
- cotangent: bfloat16 [2048, 8192], P('chan', 'seq'), may hold values from -6 to 6
- filter_taps: float32 [2048, 8192], P('chan', 'seq'), may hold values from -0.0625 to 0.0625
- skip_gain: float32 [2048], P('chan'), may hold values from -4 to 4
Outputs:
- output: bfloat16 [2048, 8192], P('chan', 'seq')
- d_post: bfloat16 [2048, 8192], P('chan', 'seq')
- d_pre: bfloat16 [2048, 8192], P('chan', 'seq')
- d_signal: bfloat16 [2048, 8192], P('chan', 'seq')
- d_skip: float32 [2048], P('chan')
- d_filter: float32 [2048, 8192], P('chan', 'seq')
The draws below stay inside these ranges and needn't reach their ends.
All inputs are finite; a program needn't handle non-finite values.
Results may differ from the reference program's by a relative error of at most 0.004.
Values sent between devices are 32-bit elements; how exact they have to be, the bound alone decides.
A program may use at most 64 MiB of HBM per device.

```python
import jax
import jax.numpy as jnp

CHANNELS = 2048
TOKENS = 8192


def steps_of(stream_key, dims, split, smallest, high):
    def one(dim, shards_of):
        heights = jax.random.uniform(jax.random.fold_in(jax.random.fold_in(stream_key, 6), dim), (shards_of,), jnp.float32, smallest / len(split), high / len(split))
        return jnp.repeat(jnp.exp(heights), dims[dim] // shards_of).reshape((-1,) + (1,) * (len(dims) - dim - 1))

    gain = one(*split[0])
    for cut in split[1:]:
        gain = gain * one(*cut)
    return gain


def gaussian(rng, shape, width, limit, shards=(), held_as=jnp.bfloat16):
    array = width * jax.random.normal(rng, shape, jnp.float32)
    if shards:
        array = array * steps_of(rng, shape, shards, -0.22, 0.18)
    return jnp.clip(array, -limit, limit).astype(held_as)


def setup_inputs(seed: int = 0) -> dict:
    seeds = jax.random.split(jax.random.key(seed), 7)
    post_gate = gaussian(seeds[0], (CHANNELS, TOKENS), 1.0, 6.0, ((0, 32), (1, 8)))
    pre_gate = gaussian(seeds[1], (CHANNELS, TOKENS), 1.0, 6.0, ((0, 32), (1, 8)))
    signal = gaussian(seeds[2], (CHANNELS, TOKENS), 1.0, 6.0, ((0, 32), (1, 8)))
    cotangent = gaussian(seeds[3], (CHANNELS, TOKENS), 1.0, 6.0, ((0, 32), (1, 8)))
    filter_taps = gaussian(seeds[4], (CHANNELS, TOKENS), TOKENS ** -0.5, 0.0625, ((0, 32), (1, 8)), jnp.float32)
    skip_gain = gaussian(seeds[5], (CHANNELS,), 1.0, 4.0, ((0, 32),), jnp.float32)
    return {"post_gate": post_gate, "pre_gate": pre_gate, "signal": signal, "cotangent": cotangent, "filter_taps": filter_taps, "skip_gain": skip_gain}


def spectra(values):
    return jnp.fft.rfft(values, n=2 * TOKENS, axis=1)


def to_time(spectrum):
    return jnp.fft.irfft(spectrum, n=2 * TOKENS, axis=1)[:, :TOKENS].astype(jnp.float32)


def reference(post_gate, pre_gate, signal, cotangent, filter_taps, skip_gain):
    post_f = post_gate.astype(jnp.float32)
    pre_f = pre_gate.astype(jnp.float32)
    signal_f = signal.astype(jnp.float32)
    gated = pre_f * signal_f
    filter_spec = spectra(filter_taps)
    gated_spec = spectra(gated)
    conv_part = to_time(filter_spec * gated_spec)
    conved = conv_part + skip_gain[:, None] * gated
    output = (post_f * conved).astype(jnp.bfloat16)
    grad_f = cotangent.astype(jnp.float32)
    d_post = (grad_f * conved).astype(jnp.bfloat16)
    d_conved = grad_f * post_f
    d_spec = spectra(d_conved)
    d_gated = to_time(jnp.conj(filter_spec) * d_spec) + skip_gain[:, None] * d_conved
    d_pre = (d_gated * signal_f).astype(jnp.bfloat16)
    d_signal = (d_gated * pre_f).astype(jnp.bfloat16)
    d_filter = to_time(jnp.conj(gated_spec) * d_spec) / (TOKENS ** 0.5)
    d_skip = jnp.sum(d_conved * gated, axis=1) / (TOKENS ** 0.5)
    return output, d_post, d_pre, d_signal, d_skip, d_filter
```

```python
import functools
import math

import jax
import jax.numpy as jnp
import numpy as np
from jax import lax
from jax.experimental import pallas as pl
from jax.experimental.pallas import tpu as pltpu
from jax.sharding import PartitionSpec as P

LANES = 128
SUB = 8
F32 = jnp.float32
BF16 = jnp.bfloat16


def halves(table):
    high = table.astype(jnp.bfloat16)
    low = (table - high.astype(np.float64)).astype(jnp.bfloat16)
    return high, low


def tables(rows, padded):
    a = np.arange(rows)[:, None]
    b = np.arange(rows)[None, :] + 0.5
    theta = 2.0 * math.pi * a * b / (2 * rows)
    first = np.concatenate([np.cos(theta).T, -np.sin(theta).T], axis=0)
    last = np.concatenate([np.cos(theta), np.sin(theta)], axis=1) * (2.0 / padded)
    r = np.arange(LANES)
    phi = 2.0 * math.pi * (np.arange(rows)[:, None] + 0.5) * r[None, :] / padded
    turn = np.stack([np.cos(phi), -np.sin(phi)]).astype(np.float32)
    psi = 2.0 * math.pi * np.outer(r, r) / LANES
    cos_m, sin_m = np.cos(psi), np.sin(psi)
    mid = np.block([[cos_m, -sin_m], [sin_m, cos_m]])
    f_hi, f_lo = halves(first)
    m_hi, m_lo = halves(mid)
    l_hi, l_lo = halves(last)
    return (
        np.concatenate([f_hi, f_hi, f_lo], axis=1),
        np.concatenate([m_hi, m_hi, m_lo], axis=0),
        np.concatenate([l_hi, l_hi, l_lo], axis=1),
        turn,
    )


def split(value, axis):
    high = value.astype(BF16)
    low = (value - high.astype(F32)).astype(BF16)
    return jnp.concatenate([high, low, high], axis=axis)


def dot(left, right):
    return jnp.dot(left, right, preferred_element_type=F32)


def kernel(
    n, chunks,
    post, pre, sig, cot, taps, skip, first, mid, last, turn,
    o_out, o_post, o_pre, o_sig, o_skip, o_taps,
    sbuf, rbuf, obuf, gbuf, dsum, dgot,
    self_sem, s_in, r_in, s_out, r_out, s_sum, r_sum,
):
    me = lax.axis_index("seq")
    chans, length = taps.shape
    blocks = length // LANES
    own = chans // n
    rows = n * blocks
    per = own // chunks
    step = per * blocks
    scale = 1.0 / math.sqrt(n * length)

    barrier = pltpu.get_barrier_semaphore()
    for k in range(1, n):
        pl.semaphore_signal(barrier, inc=1, device_id={"seq": lax.rem(me + k, n)})

    for pair in range(n // 2):
        for q in range(blocks):
            at = (slice(2 * SUB * pair, 2 * SUB * (pair + 1)), slice(LANES * q, LANES * (q + 1)))
            gated = pre[at].astype(F32) * sig[at].astype(F32)
            slope = cot[at].astype(F32) * post[at].astype(F32)
            tap = taps[at]
            for half in range(2):
                cut = slice(SUB * half, SUB * (half + 1))
                to = (2 * pair + half, pl.ds(q, SUB, stride=blocks), slice(None))
                sbuf[(0,) + to] = tap[cut]
                sbuf[(1,) + to] = gated[cut]
                sbuf[(2,) + to] = slope[cut]

    pl.semaphore_wait(barrier, n - 1)

    def inward(c, k):
        part = pl.ds(pl.multiple_of(c * step, step), step)
        return pltpu.make_async_remote_copy(
            src_ref=sbuf.at[:, lax.rem(me + k, n), part],
            dst_ref=rbuf.at[:, me, part],
            send_sem=s_in.at[c, k], recv_sem=r_in.at[c, k],
            device_id={"seq": lax.rem(me + k, n)},
        )

    def outward(c, k):
        part = pl.ds(pl.multiple_of(c * step, step), step)
        return pltpu.make_async_remote_copy(
            src_ref=obuf.at[:, lax.rem(me + k, n), part],
            dst_ref=gbuf.at[:, me, part],
            send_sem=s_out.at[c, k], recv_sem=r_out.at[c, k],
            device_id={"seq": lax.rem(me + k, n)},
        )

    def summed(k):
        return pltpu.make_async_remote_copy(
            src_ref=dsum, dst_ref=dgot.at[me],
            send_sem=s_sum.at[k], recv_sem=r_sum.at[k],
            device_id={"seq": lax.rem(me + k, n)},
        )

    def mine(which, c):
        part = pl.ds(pl.multiple_of(c * step, step), step)
        src, dst = ((sbuf, rbuf), (obuf, gbuf))[which]
        return pltpu.make_async_copy(src.at[:, me, part], dst.at[:, me, part], self_sem.at[which, c])

    for c in range(chunks):
        for k in range(1, n):
            inward(c, k).start()
        mine(0, c).start()

    def chunk(c, carry):
        for k in range(1, n):
            inward(c, k).wait()
        mine(0, c).wait()
        base = pl.multiple_of(c * step, step)
        grown = []
        for f in range(3):
            xs = []
            for i in range(per):
                xs.append(rbuf[f, :, pl.ds(base + i * blocks, blocks), :].reshape(rows, LANES))
            if f == 1:
                gates = xs
            if f == 2:
                for i in range(per):
                    dsum[pl.ds(c * per + i, 1), :] = jnp.sum(gates[i] * xs[i], axis=0, keepdims=True)
            x = jnp.concatenate(xs, axis=1)
            y = dot(first[...], split(x, 0))
            for i in range(per):
                cut = slice(LANES * i, LANES * (i + 1))
                re, im = y[:rows, cut], y[rows:, cut]
                grown.append(jnp.concatenate([re * turn[0] - im * turn[1], re * turn[1] + im * turn[0]], axis=1))
        spec = dot(split(jnp.concatenate(grown, axis=0), 1), mid[...])
        prods = [[], [], []]
        for i in range(per):
            parts = []
            for f in range(3):
                top = (f * per + i) * rows
                parts.append((spec[top:top + rows, :LANES], spec[top:top + rows, LANES:]))
            (hr, hi), (gr, gi), (dr, di) = parts
            prods[0].append(jnp.concatenate([hr * gr - hi * gi, -(hr * gi + hi * gr)], axis=1))
            prods[1].append(jnp.concatenate([hr * dr + hi * di, hi * dr - hr * di], axis=1))
            prods[2].append(jnp.concatenate([gr * dr + gi * di, gi * dr - gr * di], axis=1))
        back = dot(split(jnp.concatenate(prods[0] + prods[1] + prods[2], axis=0), 1), mid[...])
        for f in range(3):
            cols = []
            for i in range(per):
                top = (f * per + i) * rows
                re, im = back[top:top + rows, :LANES], back[top:top + rows, LANES:]
                cols.append(jnp.concatenate([re * turn[0] - im * turn[1], re * turn[1] + im * turn[0]], axis=0))
            out = dot(last[...], split(jnp.concatenate(cols, axis=1), 0))
            for i in range(per):
                obuf[f, :, pl.ds(base + i * blocks, blocks), :] = out[:, LANES * i:LANES * (i + 1)].reshape(n, blocks, LANES)
        for k in range(1, n):
            outward(c, k).start()
        mine(1, c).start()
        return carry

    lax.fori_loop(0, chunks, chunk, 0)
    for k in range(1, n):
        summed(k).start()

    lane = lax.broadcasted_iota(jnp.int32, (chans, chans), 1)
    row = lax.broadcasted_iota(jnp.int32, (chans, chans), 0)
    gain = jnp.sum(jnp.where(lane == row, jnp.broadcast_to(skip[...], (chans, chans)), 0.0), axis=1, keepdims=True)

    for c in range(chunks):
        for k in range(1, n):
            outward(c, k).wait()
        mine(1, c).wait()
    for k in range(1, n):
        summed(k).wait()
    dgot[me] = dsum[...]

    for pair in range(n // 2):
        down = slice(2 * SUB * pair, 2 * SUB * (pair + 1))
        col = jnp.broadcast_to(gain[down], (2 * SUB, LANES))
        for q in range(blocks):
            at = (down, slice(LANES * q, LANES * (q + 1)))
            got = []
            for f in range(3):
                got.append(jnp.concatenate([gbuf[f, 2 * pair + half, pl.ds(q, SUB, stride=blocks), :] for half in range(2)], axis=0))
            post_f, pre_f = post[at].astype(F32), pre[at].astype(F32)
            sig_f, cot_f = sig[at].astype(F32), cot[at].astype(F32)
            conved = got[0] + col * (pre_f * sig_f)
            o_out[at] = (post_f * conved).astype(BF16)
            o_post[at] = (cot_f * conved).astype(BF16)
            d_gated = got[1] + col * (cot_f * post_f)
            o_pre[at] = (d_gated * sig_f).astype(BF16)
            o_sig[at] = (d_gated * pre_f).astype(BF16)
            o_taps[at] = got[2] * scale
    total = jnp.sum(dgot[...].reshape(chans, LANES), axis=1, keepdims=True) * scale
    o_skip[...] = jnp.sum(jnp.where(lane == row, jnp.broadcast_to(total, (chans, chans)), 0.0), axis=0, keepdims=True)


def solution(mesh):
    n = mesh.shape["seq"]
    chunks = 4

    def shards(post_gate, pre_gate, signal, cotangent, filter_taps, skip_gain):
        chans, length = filter_taps.shape
        blocks = length // LANES
        own = chans // n
        first, mid, last, turn = tables(n * blocks, 2 * n * length)
        vmem = pl.BlockSpec(memory_space=pltpu.VMEM)
        small = jax.ShapeDtypeStruct((chans, length), BF16)
        buf = pltpu.VMEM((3, n, own * blocks, LANES), F32)
        sem = pltpu.SemaphoreType.DMA((chunks, n))
        outs = pl.pallas_call(
            functools.partial(kernel, n, chunks),
            out_shape=(small, small, small, small, jax.ShapeDtypeStruct((1, chans), F32), jax.ShapeDtypeStruct((chans, length), F32)),
            in_specs=[vmem] * 10,
            out_specs=[vmem] * 6,
            scratch_shapes=[
                buf, buf, buf, buf,
                pltpu.VMEM((own, LANES), F32), pltpu.VMEM((n, own, LANES), F32),
                pltpu.SemaphoreType.DMA((2, chunks)), sem, sem, sem, sem,
                pltpu.SemaphoreType.DMA((n,)), pltpu.SemaphoreType.DMA((n,)),
            ],
            compiler_params=pltpu.CompilerParams(collective_id=0, has_side_effects=True, vmem_limit_bytes=48 << 20),
        )(post_gate, pre_gate, signal, cotangent, filter_taps, skip_gain.reshape(1, chans), first, mid, last, turn)
        return outs[0], outs[1], outs[2], outs[3], outs[4].reshape(chans), outs[5]

    return jax.shard_map(
        shards,
        mesh=mesh,
        in_specs=(P("chan", "seq"),) * 5 + (P("chan"),),
        out_specs=(P("chan", "seq"),) * 4 + (P("chan"), P("chan", "seq")),
        check_vma=False,
    )
```

```python
import functools
import math

import jax
import jax.numpy as jnp
import numpy as np
from jax import lax
from jax.experimental import pallas as pl
from jax.experimental.pallas import tpu as pltpu
from jax.sharding import PartitionSpec as P

LANES = 128
SUB = 8
F32 = jnp.float32
BF16 = jnp.bfloat16


def halves(table):
    high = table.astype(jnp.bfloat16)
    low = (table - high.astype(np.float64)).astype(jnp.bfloat16)
    return high, low


def tables(rows, padded):
    a = np.arange(rows)[:, None]
    b = np.arange(rows)[None, :] + 0.5
    theta = 2.0 * math.pi * a * b / (2 * rows)
    first = np.concatenate([np.cos(theta).T, -np.sin(theta).T], axis=0)
    last = np.concatenate([np.cos(theta), np.sin(theta)], axis=1) * (2.0 / padded)
    r = np.arange(LANES)
    phi = 2.0 * math.pi * (np.arange(rows)[:, None] + 0.5) * r[None, :] / padded
    turn = np.stack([np.cos(phi), -np.sin(phi)]).astype(np.float32)
    psi = 2.0 * math.pi * np.outer(r, r) / LANES
    cos_m, sin_m = np.cos(psi), np.sin(psi)
    mid = np.block([[cos_m, -sin_m], [sin_m, cos_m]])
    f_hi, f_lo = halves(first)
    m_hi, m_lo = halves(mid)
    l_hi, l_lo = halves(last)
    return (
        np.concatenate([f_hi, f_hi, f_lo], axis=1),
        np.concatenate([m_hi, m_hi, m_lo], axis=0),
        np.concatenate([l_hi, l_hi, l_lo], axis=1),
        turn,
    )


def split(value, axis):
    high = value.astype(BF16)
    low = (value - high.astype(F32)).astype(BF16)
    return jnp.concatenate([high, low, high], axis=axis)


def dot(left, right):
    return jnp.dot(left, right, preferred_element_type=F32)


def fill(pairs, sems):
    copies = [pltpu.make_async_copy(src, dst, sems.at[i]) for i, (src, dst) in enumerate(pairs)]
    for copy in copies:
        copy.start()
    return copies


def exchange(
    n, chunks,
    h_post, h_pre, h_sig, h_cot, h_taps, h_first, h_mid, h_last, h_turn, h_skip,
    gbuf, dgot, post, pre, sig, cot, skip,
    taps, first, mid, last, turn, sbuf, rbuf, obuf, dsum,
    load_sem, self_sem, s_in, r_in, s_out, r_out, s_sum, r_sum,
):
    me = lax.axis_index("seq")
    chans, length = taps.shape
    blocks = length // LANES
    own = chans // n
    rows = n * blocks
    per = own // chunks
    step = per * blocks

    barrier = pltpu.get_barrier_semaphore()
    for k in range(1, n):
        pl.semaphore_signal(barrier, inc=1, device_id={"seq": lax.rem(me + k, n)})
    loads = fill(
        [(h_taps, taps), (h_pre, pre), (h_sig, sig), (h_cot, cot), (h_post, post),
         (h_first, first), (h_mid, mid), (h_turn, turn), (h_last, last), (h_skip, skip)], load_sem)
    for load in loads[:5]:
        load.wait()

    for pair in range(n // 2):
        for q in range(blocks):
            at = (slice(2 * SUB * pair, 2 * SUB * (pair + 1)), slice(LANES * q, LANES * (q + 1)))
            gated = pre[at].astype(F32) * sig[at].astype(F32)
            slope = cot[at].astype(F32) * post[at].astype(F32)
            tap = taps[at]
            for half in range(2):
                cut = slice(SUB * half, SUB * (half + 1))
                to = (2 * pair + half, pl.ds(q, SUB, stride=blocks), slice(None))
                sbuf[(0,) + to] = tap[cut]
                sbuf[(1,) + to] = gated[cut]
                sbuf[(2,) + to] = slope[cut]

    pl.semaphore_wait(barrier, n - 1)

    def inward(c, k):
        part = pl.ds(pl.multiple_of(c * step, step), step)
        return pltpu.make_async_remote_copy(
            src_ref=sbuf.at[:, lax.rem(me + k, n), part],
            dst_ref=rbuf.at[:, me, part],
            send_sem=s_in.at[c, k], recv_sem=r_in.at[c, k],
            device_id={"seq": lax.rem(me + k, n)},
        )

    def outward(c, k):
        part = pl.ds(pl.multiple_of(c * step, step), step)
        return pltpu.make_async_remote_copy(
            src_ref=obuf.at[:, lax.rem(me + k, n), part],
            dst_ref=gbuf.at[:, me, part],
            send_sem=s_out.at[c, k], recv_sem=r_out.at[c, k],
            device_id={"seq": lax.rem(me + k, n)},
        )

    def summed(k):
        return pltpu.make_async_remote_copy(
            src_ref=dsum, dst_ref=dgot.at[me],
            send_sem=s_sum.at[k], recv_sem=r_sum.at[k],
            device_id={"seq": lax.rem(me + k, n)},
        )

    def mine(which, c):
        part = pl.ds(pl.multiple_of(c * step, step), step)
        src, dst = ((sbuf, rbuf), (obuf, gbuf))[which]
        return pltpu.make_async_copy(src.at[:, me, part], dst.at[:, me, part], self_sem.at[which, c])

    for c in range(chunks):
        for k in range(1, n):
            inward(c, k).start()
        mine(0, c).start()

    for load in loads[5:]:
        load.wait()

    def chunk(c, carry):
        for k in range(1, n):
            inward(c, k).wait()
        mine(0, c).wait()
        base = pl.multiple_of(c * step, step)
        grown = []
        for f in range(3):
            xs = []
            for i in range(per):
                xs.append(rbuf[f, :, pl.ds(base + i * blocks, blocks), :].reshape(rows, LANES))
            if f == 1:
                gates = xs
            if f == 2:
                for i in range(per):
                    dsum[pl.ds(c * per + i, 1), :] = jnp.sum(gates[i] * xs[i], axis=0, keepdims=True)
            x = jnp.concatenate(xs, axis=1)
            y = dot(first[...], split(x, 0))
            for i in range(per):
                cut = slice(LANES * i, LANES * (i + 1))
                re, im = y[:rows, cut], y[rows:, cut]
                grown.append(jnp.concatenate([re * turn[0] - im * turn[1], re * turn[1] + im * turn[0]], axis=1))
        spec = dot(split(jnp.concatenate(grown, axis=0), 1), mid[...])
        prods = [[], [], []]
        for i in range(per):
            parts = []
            for f in range(3):
                top = (f * per + i) * rows
                parts.append((spec[top:top + rows, :LANES], spec[top:top + rows, LANES:]))
            (hr, hi), (gr, gi), (dr, di) = parts
            prods[0].append(jnp.concatenate([hr * gr - hi * gi, -(hr * gi + hi * gr)], axis=1))
            prods[1].append(jnp.concatenate([hr * dr + hi * di, hi * dr - hr * di], axis=1))
            prods[2].append(jnp.concatenate([gr * dr + gi * di, gi * dr - gr * di], axis=1))
        back = dot(split(jnp.concatenate(prods[0] + prods[1] + prods[2], axis=0), 1), mid[...])
        for f in range(3):
            cols = []
            for i in range(per):
                top = (f * per + i) * rows
                re, im = back[top:top + rows, :LANES], back[top:top + rows, LANES:]
                cols.append(jnp.concatenate([re * turn[0] - im * turn[1], re * turn[1] + im * turn[0]], axis=0))
            out = dot(last[...], split(jnp.concatenate(cols, axis=1), 0))
            for i in range(per):
                obuf[f, :, pl.ds(base + i * blocks, blocks), :] = out[:, LANES * i:LANES * (i + 1)].reshape(n, blocks, LANES)
        for k in range(1, n):
            outward(c, k).start()
        mine(1, c).start()
        return carry

    lax.fori_loop(0, chunks, chunk, 0)
    for k in range(1, n):
        summed(k).start()


    for c in range(chunks):
        for k in range(1, n):
            outward(c, k).wait()
        mine(1, c).wait()
    for k in range(1, n):
        summed(k).wait()
    dgot[me] = dsum[...]


def finish(n, gbuf, dgot, post, pre, sig, cot, skip, h_out, h_post, h_pre, h_sig, h_skip, h_taps,
           o_out, o_post, o_pre, o_sig, o_skip, o_taps, sems):
    chans, length = post.shape
    blocks = length // LANES
    scale = 1.0 / math.sqrt(n * length)
    lane = lax.broadcasted_iota(jnp.int32, (chans, chans), 1)
    row = lax.broadcasted_iota(jnp.int32, (chans, chans), 0)
    gain = jnp.sum(jnp.where(lane == row, jnp.broadcast_to(skip[...], (chans, chans)), 0.0), axis=1, keepdims=True)
    total = jnp.sum(dgot[...].reshape(chans, LANES), axis=1, keepdims=True) * scale
    o_skip[...] = jnp.sum(jnp.where(lane == row, jnp.broadcast_to(total, (chans, chans)), 0.0), axis=0, keepdims=True)
    stores = fill([(o_skip, h_skip)], sems.at[n // 2])
    for pair in range(n // 2):
        down = slice(2 * SUB * pair, 2 * SUB * (pair + 1))
        col = jnp.broadcast_to(gain[down], (2 * SUB, LANES))
        for q in range(blocks):
            at = (down, slice(LANES * q, LANES * (q + 1)))
            got = []
            for f in range(3):
                got.append(jnp.concatenate([gbuf[f, 2 * pair + half, pl.ds(q, SUB, stride=blocks), :] for half in range(2)], axis=0))
            post_f, pre_f = post[at].astype(F32), pre[at].astype(F32)
            sig_f, cot_f = sig[at].astype(F32), cot[at].astype(F32)
            conved = got[0] + col * (pre_f * sig_f)
            o_out[at] = (post_f * conved).astype(BF16)
            o_post[at] = (cot_f * conved).astype(BF16)
            d_gated = got[1] + col * (cot_f * post_f)
            o_pre[at] = (d_gated * sig_f).astype(BF16)
            o_sig[at] = (d_gated * pre_f).astype(BF16)
            o_taps[at] = got[2] * scale
        stores += fill([(src.at[down], dst.at[down]) for src, dst in
                        ((o_out, h_out), (o_post, h_post), (o_pre, h_pre), (o_sig, h_sig), (o_taps, h_taps))], sems.at[pair])
    for store in stores:
        store.wait()


def solution(mesh):
    n = mesh.shape["seq"]
    chunks = 4

    def shards(post_gate, pre_gate, signal, cotangent, filter_taps, skip_gain):
        chans, length = filter_taps.shape
        blocks = length // LANES
        own = chans // n
        first, mid, last, turn = tables(n * blocks, 2 * n * length)
        vmem = pl.BlockSpec(memory_space=pltpu.VMEM)
        hbm = pl.BlockSpec(memory_space=pltpu.HBM)
        half = jax.ShapeDtypeStruct((chans, length), BF16)
        full = jax.ShapeDtypeStruct((chans, length), F32)
        line = jax.ShapeDtypeStruct((1, chans), F32)
        fields = (3, n, own * blocks, LANES)
        buf = pltpu.VMEM(fields, F32)
        sem = pltpu.SemaphoreType.DMA((chunks, n))
        got = pl.pallas_call(
            functools.partial(exchange, n, chunks),
            out_shape=(jax.ShapeDtypeStruct(fields, F32), jax.ShapeDtypeStruct((n, own, LANES), F32), half, half, half, half, line),
            in_specs=[hbm] * 10,
            out_specs=[vmem] * 7,
            scratch_shapes=[
                pltpu.VMEM((chans, length), F32),
                pltpu.VMEM(first.shape, BF16), pltpu.VMEM(mid.shape, BF16), pltpu.VMEM(last.shape, BF16), pltpu.VMEM(turn.shape, F32),
                buf, buf, buf,
                pltpu.VMEM((own, LANES), F32),
                pltpu.SemaphoreType.DMA((10,)),
                pltpu.SemaphoreType.DMA((2, chunks)), sem, sem, sem, sem,
                pltpu.SemaphoreType.DMA((n,)), pltpu.SemaphoreType.DMA((n,)),
            ],
            compiler_params=pltpu.CompilerParams(collective_id=0, has_side_effects=True, vmem_limit_bytes=32 << 20),
        )(*[pltpu.with_memory_space_constraint(x, pltpu.HBM) for x in (
            post_gate, pre_gate, signal, cotangent, filter_taps, first, mid, last, turn, skip_gain.reshape(1, chans))])
        outs = pl.pallas_call(
            functools.partial(finish, n),
            out_shape=(half, half, half, half, line, full),
            in_specs=[vmem] * 7,
            out_specs=[hbm] * 6,
            scratch_shapes=[pltpu.VMEM((chans, length), BF16)] * 4 + [
                pltpu.VMEM((1, chans), F32), pltpu.VMEM((chans, length), F32), pltpu.SemaphoreType.DMA((n // 2 + 1, 5))],
            compiler_params=pltpu.CompilerParams(vmem_limit_bytes=32 << 20),
        )(*got)
        return outs[0], outs[1], outs[2], outs[3], outs[4].reshape(chans), outs[5]

    return jax.shard_map(
        shards,
        mesh=mesh,
        in_specs=(P("chan", "seq"),) * 5 + (P("chan"),),
        out_specs=(P("chan", "seq"),) * 4 + (P("chan"), P("chan", "seq")),
        check_vma=False,
    )
```

```python
import functools
import math

import jax
import jax.numpy as jnp
import numpy as np
from jax import lax
from jax.experimental import pallas as pl
from jax.experimental.pallas import tpu as pltpu
from jax.sharding import PartitionSpec as P

LANES = 128
SUB = 8
F32 = jnp.float32
BF16 = jnp.bfloat16


def halves(table):
    high = table.astype(jnp.bfloat16)
    low = (table - high.astype(np.float64)).astype(jnp.bfloat16)
    return high, low


def tables(rows, padded):
    a = np.arange(rows)[:, None]
    b = np.arange(rows)[None, :] + 0.5
    theta = 2.0 * math.pi * a * b / (2 * rows)
    first = np.concatenate([np.cos(theta).T, -np.sin(theta).T], axis=0)
    last = np.concatenate([np.cos(theta), np.sin(theta)], axis=1) * (2.0 / padded)
    r = np.arange(LANES)
    phi = 2.0 * math.pi * (np.arange(rows)[:, None] + 0.5) * r[None, :] / padded
    turn = np.stack([np.cos(phi), -np.sin(phi)]).astype(np.float32)
    psi = 2.0 * math.pi * np.outer(r, r) / LANES
    cos_m, sin_m = np.cos(psi), np.sin(psi)
    mid = np.block([[cos_m, -sin_m], [sin_m, cos_m]])
    f_hi, f_lo = halves(first)
    m_hi, m_lo = halves(mid)
    l_hi, l_lo = halves(last)
    return (
        np.concatenate([f_hi, f_hi, f_lo], axis=1),
        np.concatenate([m_hi, m_hi, m_lo], axis=0),
        np.concatenate([l_hi, l_hi, l_lo], axis=1),
        turn,
    )


def split(value, axis):
    high = value.astype(BF16)
    low = (value - high.astype(F32)).astype(BF16)
    return jnp.concatenate([high, low, high], axis=axis)


def dot(left, right):
    return jnp.dot(left, right, preferred_element_type=F32)


def fill(pairs, sems):
    copies = [pltpu.make_async_copy(src, dst, sems.at[i]) for i, (src, dst) in enumerate(pairs)]
    for copy in copies:
        copy.start()
    return copies


def exchange(
    n, chunks,
    h_post, h_pre, h_sig, h_cot, h_taps, h_first, h_mid, h_last, h_turn, h_skip,
    o_out, o_post, o_pre, o_sig, o_skip, o_taps,
    post, pre, sig, cot, taps, first, mid, last, turn, skip, sbuf, rbuf, obuf, gbuf, dsum, dgot,
    load_sem, self_sem, s_in, r_in, s_out, r_out, s_sum, r_sum,
):
    me = lax.axis_index("seq")
    chans, length = taps.shape
    blocks = length // LANES
    rows = n * blocks
    group = chans // chunks
    per = group // n
    step = per * blocks
    scale = 1.0 / math.sqrt(n * length)

    barrier = pltpu.get_barrier_semaphore()
    for k in range(1, n):
        pl.semaphore_signal(barrier, inc=1, device_id={"seq": lax.rem(me + k, n)})
    loads = fill(
        [(h_taps, taps), (h_pre, pre), (h_sig, sig), (h_cot, cot), (h_post, post),
         (h_first, first), (h_mid, mid), (h_turn, turn), (h_last, last), (h_skip, skip)], load_sem)
    for load in loads[:5]:
        load.wait()

    def peer(k):
        return lax.rem(me + k, n)

    def rows_of(t):
        return pl.ds(pl.multiple_of(t * step, step), step)

    def inward(c, k):
        return pltpu.make_async_remote_copy(
            src_ref=sbuf.at[:, c, rows_of(peer(k))], dst_ref=rbuf.at[:, c, me],
            send_sem=s_in.at[c, k], recv_sem=r_in.at[c, k], device_id={"seq": peer(k)},
        )

    def outward(c, k):
        return pltpu.make_async_remote_copy(
            src_ref=obuf.at[:, c, peer(k)], dst_ref=gbuf.at[:, c, rows_of(me)],
            send_sem=s_out.at[c, k], recv_sem=r_out.at[c, k], device_id={"seq": peer(k)},
        )

    def summed(k):
        return pltpu.make_async_remote_copy(
            src_ref=dsum, dst_ref=dgot.at[me],
            send_sem=s_sum.at[k], recv_sem=r_sum.at[k], device_id={"seq": peer(k)},
        )

    def kept_in(c):
        return pltpu.make_async_copy(sbuf.at[:, c, rows_of(me)], rbuf.at[:, c, me], self_sem.at[0, c])

    def kept_out(c):
        return pltpu.make_async_copy(obuf.at[:, c, me], gbuf.at[:, c, rows_of(me)], self_sem.at[1, c])

    for c in range(chunks):
        for q in range(blocks):
            at = (slice(group * c, group * (c + 1)), slice(LANES * q, LANES * (q + 1)))
            gated = pre[at].astype(F32) * sig[at].astype(F32)
            slope = cot[at].astype(F32) * post[at].astype(F32)
            for f, value in enumerate((taps[at], gated, slope)):
                for half in range(group // SUB):
                    sbuf[f, c, pl.ds(q + half * SUB * blocks, SUB, stride=blocks), :] = value[SUB * half:SUB * (half + 1)]
        if c == 0:
            pl.semaphore_wait(barrier, n - 1)
        for k in range(1, n):
            inward(c, k).start()
        kept_in(c).start()
    for load in loads[5:]:
        load.wait()

    def chunk(c, carry):
        for k in range(1, n):
            inward(c, k).wait()
        kept_in(c).wait()
        grown = []
        gates = []
        for f in range(3):
            xs = []
            for i in range(per):
                xs.append(rbuf[f, c, :, blocks * i:blocks * (i + 1), :].reshape(rows, LANES))
            if f == 1:
                gates = xs
            if f == 2:
                for i in range(per):
                    dsum[pl.ds(c * per + i, 1), :] = jnp.sum(gates[i] * xs[i], axis=0, keepdims=True)
            y = dot(first[...], split(jnp.concatenate(xs, axis=1), 0))
            for i in range(per):
                cut = slice(LANES * i, LANES * (i + 1))
                re, im = y[:rows, cut], y[rows:, cut]
                grown.append(jnp.concatenate([re * turn[0] - im * turn[1], re * turn[1] + im * turn[0]], axis=1))

        @pl.when(c == chunks - 1)
        def _():
            for k in range(1, n):
                summed(k).start()

        spec = dot(split(jnp.concatenate(grown, axis=0), 1), mid[...])
        prods = [[], [], []]
        for i in range(per):
            parts = []
            for f in range(3):
                top = (f * per + i) * rows
                parts.append((spec[top:top + rows, :LANES], spec[top:top + rows, LANES:]))
            (hr, hi), (gr, gi), (dr, di) = parts
            prods[0].append(jnp.concatenate([hr * gr - hi * gi, -(hr * gi + hi * gr)], axis=1))
            prods[1].append(jnp.concatenate([hr * dr + hi * di, hi * dr - hr * di], axis=1))
            prods[2].append(jnp.concatenate([gr * dr + gi * di, gi * dr - gr * di], axis=1))
        back = dot(split(jnp.concatenate(prods[0] + prods[1] + prods[2], axis=0), 1), mid[...])
        for f in range(3):
            cols = []
            for i in range(per):
                top = (f * per + i) * rows
                re, im = back[top:top + rows, :LANES], back[top:top + rows, LANES:]
                cols.append(jnp.concatenate([re * turn[0] - im * turn[1], re * turn[1] + im * turn[0]], axis=0))
            out = dot(last[...], split(jnp.concatenate(cols, axis=1), 0))
            for i in range(per):
                obuf[f, c, :, blocks * i:blocks * (i + 1), :] = out[:, LANES * i:LANES * (i + 1)].reshape(n, blocks, LANES)
        for k in range(1, n):
            outward(c, k).start()
        kept_out(c).start()
        return carry

    lax.fori_loop(0, chunks, chunk, 0)

    dgot[me] = dsum[...]
    for k in range(1, n):
        summed(k).wait()
    lane = lax.broadcasted_iota(jnp.int32, (chans, chans), 1)
    row = lax.broadcasted_iota(jnp.int32, (chans, chans), 0)
    gain = jnp.sum(jnp.where(lane == row, jnp.broadcast_to(skip[...], (chans, chans)), 0.0), axis=1, keepdims=True)
    own = chunks * per
    place = (row % own) // per * group + row // own * per + row % per
    total = jnp.sum(dgot[...].reshape(chans, LANES), axis=1, keepdims=True) * scale
    o_skip[...] = jnp.sum(jnp.where(lane == place, jnp.broadcast_to(total, (chans, chans)), 0.0), axis=0, keepdims=True)

    for c in range(chunks):
        down = slice(group * c, group * (c + 1))
        col = jnp.broadcast_to(gain[down], (group, LANES))
        for k in range(1, n):
            outward(c, k).wait()
        kept_out(c).wait()
        for q in range(blocks):
            at = (down, slice(LANES * q, LANES * (q + 1)))
            got = []
            for f in range(3):
                got.append(jnp.concatenate(
                    [gbuf[f, c, pl.ds(q + half * SUB * blocks, SUB, stride=blocks), :] for half in range(group // SUB)], axis=0))
            post_f, pre_f = post[at].astype(F32), pre[at].astype(F32)
            sig_f, cot_f = sig[at].astype(F32), cot[at].astype(F32)
            conved = got[0] + col * (pre_f * sig_f)
            o_out[at] = (post_f * conved).astype(BF16)
            o_post[at] = (cot_f * conved).astype(BF16)
            d_gated = got[1] + col * (cot_f * post_f)
            o_pre[at] = (d_gated * sig_f).astype(BF16)
            o_sig[at] = (d_gated * pre_f).astype(BF16)
            o_taps[at] = got[2] * scale


def store(*refs):
    half = len(refs) // 2
    for copy in fill(list(zip(refs[:half], refs[half:-1])), refs[-1]):
        copy.wait()


def solution(mesh):
    n = mesh.shape["seq"]
    chunks = 4

    def shards(post_gate, pre_gate, signal, cotangent, filter_taps, skip_gain):
        chans, length = filter_taps.shape
        blocks = length // LANES
        own = chans // n
        per = own // chunks
        first, mid, last, turn = tables(n * blocks, 2 * n * length)
        vmem = pl.BlockSpec(memory_space=pltpu.VMEM)
        hbm = pl.BlockSpec(memory_space=pltpu.HBM)
        half = jax.ShapeDtypeStruct((chans, length), BF16)
        results = (half, half, half, half, jax.ShapeDtypeStruct((1, chans), F32), jax.ShapeDtypeStruct((chans, length), F32))
        gates = pltpu.VMEM((chans, length), BF16)
        flat = pltpu.VMEM((3, chunks, n * per * blocks, LANES), F32)
        cut = pltpu.VMEM((3, chunks, n, per * blocks, LANES), F32)
        sem = pltpu.SemaphoreType.DMA((chunks, n))
        operands = (post_gate, pre_gate, signal, cotangent, filter_taps, first, mid, last, turn, skip_gain.reshape(1, chans))
        got = pl.pallas_call(
            functools.partial(exchange, n, chunks),
            out_shape=results,
            in_specs=[hbm] * 10,
            out_specs=[vmem] * 6,
            scratch_shapes=[
                gates, gates, gates, gates, pltpu.VMEM((chans, length), F32),
                pltpu.VMEM(first.shape, BF16), pltpu.VMEM(mid.shape, BF16), pltpu.VMEM(last.shape, BF16), pltpu.VMEM(turn.shape, F32),
                pltpu.VMEM((1, chans), F32),
                flat, cut, cut, flat,
                pltpu.VMEM((own, LANES), F32), pltpu.VMEM((n, own, LANES), F32),
                pltpu.SemaphoreType.DMA((10,)),
                pltpu.SemaphoreType.DMA((2, chunks)), sem, sem, sem, sem,
                pltpu.SemaphoreType.DMA((n,)), pltpu.SemaphoreType.DMA((n,)),
            ],
            compiler_params=pltpu.CompilerParams(collective_id=0, has_side_effects=True, vmem_limit_bytes=32 << 20),
        )(*[pltpu.with_memory_space_constraint(x, pltpu.HBM) for x in operands])
        outs = pl.pallas_call(
            store,
            out_shape=results,
            in_specs=[vmem] * 6,
            out_specs=[hbm] * 6,
            scratch_shapes=[pltpu.SemaphoreType.DMA((6,))],
            compiler_params=pltpu.CompilerParams(vmem_limit_bytes=32 << 20),
        )(*got)
        return outs[0], outs[1], outs[2], outs[3], outs[4].reshape(chans), outs[5]

    return jax.shard_map(
        shards,
        mesh=mesh,
        in_specs=(P("chan", "seq"),) * 5 + (P("chan"),),
        out_specs=(P("chan", "seq"),) * 4 + (P("chan"), P("chan", "seq")),
        check_vma=False,
    )
```

```python
import functools
import math

import jax
import jax.numpy as jnp
import numpy as np
from jax import lax
from jax.experimental import pallas as pl
from jax.experimental.pallas import tpu as pltpu
from jax.sharding import PartitionSpec as P

LANES = 128
SUB = 8
F32 = jnp.float32
BF16 = jnp.bfloat16


def halves(table):
    high = table.astype(jnp.bfloat16)
    low = (table - high.astype(np.float64)).astype(jnp.bfloat16)
    return high, low


def tables(rows, padded):
    a = np.arange(rows)[:, None]
    b = np.arange(rows)[None, :] + 0.5
    theta = 2.0 * math.pi * a * b / (2 * rows)
    first = np.concatenate([np.cos(theta).T, -np.sin(theta).T], axis=0)
    last = np.concatenate([np.cos(theta), np.sin(theta)], axis=1) * (2.0 / padded)
    r = np.arange(LANES)
    phi = 2.0 * math.pi * (np.arange(rows)[:, None] + 0.5) * r[None, :] / padded
    turn = np.stack([np.cos(phi), -np.sin(phi)]).astype(np.float32)
    psi = 2.0 * math.pi * np.outer(r, r) / LANES
    cos_m, sin_m = np.cos(psi), np.sin(psi)
    mid = np.block([[cos_m, -sin_m], [sin_m, cos_m]])
    f_hi, f_lo = halves(first)
    m_hi, m_lo = halves(mid)
    l_hi, l_lo = halves(last)
    return (
        np.concatenate([f_hi, f_hi, f_lo], axis=1),
        np.concatenate([m_hi, m_hi, m_lo], axis=0),
        np.concatenate([l_hi, l_hi, l_lo], axis=1),
        turn,
    )


def split(value, axis):
    high = value.astype(BF16)
    low = (value - high.astype(F32)).astype(BF16)
    return jnp.concatenate([high, low, high], axis=axis)


def dot(left, right):
    return jnp.dot(left, right, preferred_element_type=F32)


def fill(pairs, sems):
    copies = [pltpu.make_async_copy(src, dst, sems.at[i]) for i, (src, dst) in enumerate(pairs)]
    for copy in copies:
        copy.start()
    return copies


def exchange(
    n, chunks, join,
    h_post, h_pre, h_sig, h_cot, h_taps, h_first, h_mid, h_last, h_turn, h_skip,
    o_out, o_post, o_pre, o_sig, o_skip, o_taps,
    post, pre, sig, cot, taps, first, mid, last, turn, skip, sbuf, rbuf, obuf, gbuf, dsum, dgot, sums,
    load_sem, self_sem, s_in, r_in, s_out, r_out, s_sum, r_sum,
):
    me = lax.axis_index("seq")
    chans, length = taps.shape
    blocks = length // LANES
    rows = n * blocks
    group = chans // chunks
    per = group // n
    step = per * blocks
    tall = 3 * step
    scale = 1.0 / math.sqrt(n * length)

    barrier = pltpu.get_barrier_semaphore()
    for k in range(1, n):
        pl.semaphore_signal(barrier, inc=1, device_id={"seq": lax.rem(me + k, n)})
    loads = fill(
        [(h_taps, taps), (h_pre, pre), (h_sig, sig), (h_cot, cot), (h_post, post),
         (h_first, first), (h_mid, mid), (h_turn, turn), (h_last, last), (h_skip, skip)], load_sem)
    for load in loads[:5]:
        load.wait()

    def peer(k):
        return lax.rem(me + k, n)

    def wide_of(t):
        return pl.ds(pl.multiple_of(t * join * tall, join * tall), join * tall)

    def rows_of(t):
        return pl.ds(pl.multiple_of(t * tall, tall), tall)

    def spread(f, i, q, more=0, wide=1):
        return pl.ds(more * tall + f * step + i * blocks + q, n, stride=wide * tall)

    def inward(c, k):
        return pltpu.make_async_remote_copy(
            src_ref=sbuf.at[c, rows_of(peer(k))], dst_ref=rbuf.at[c, me],
            send_sem=s_in.at[c, k], recv_sem=r_in.at[c, k], device_id={"seq": peer(k)},
        )

    def outward(c, k):
        return pltpu.make_async_remote_copy(
            src_ref=obuf.at[c, peer(k)], dst_ref=gbuf.at[c, wide_of(me)],
            send_sem=s_out.at[c, k], recv_sem=r_out.at[c, k], device_id={"seq": peer(k)},
        )

    def summed(k):
        return pltpu.make_async_remote_copy(
            src_ref=dsum, dst_ref=dgot.at[me],
            send_sem=s_sum.at[k], recv_sem=r_sum.at[k], device_id={"seq": peer(k)},
        )

    def kept_in(c):
        return pltpu.make_async_copy(sbuf.at[c, rows_of(me)], rbuf.at[c, me], self_sem.at[0, c])

    def kept_out(c):
        return pltpu.make_async_copy(obuf.at[c, me], gbuf.at[c, wide_of(me)], self_sem.at[1, c])

    for c in range(chunks):
        for q in range(blocks):
            at = (slice(group * c, group * (c + 1)), slice(LANES * q, LANES * (q + 1)))
            gated = pre[at].astype(F32) * sig[at].astype(F32)
            slope = cot[at].astype(F32) * post[at].astype(F32)
            for f, value in enumerate((taps[at], gated, slope)):
                for i in range(per):
                    sbuf[c, spread(f, i, q), :] = value[n * i:n * (i + 1)]
        if c == 0:
            pl.semaphore_wait(barrier, n - 1)
        for k in range(1, n):
            inward(c, k).start()
        kept_in(c).start()
    for load in loads[5:]:
        load.wait()

    spot = lax.broadcasted_iota(jnp.int32, (1, LANES), 1)
    dsum[...] = jnp.zeros_like(dsum)

    def chunk(c, carry):
        for k in range(1, n):
            inward(c, k).wait()
        kept_in(c).wait()
        grown = []
        gates = []
        for f in range(3):
            xs = []
            for i in range(per):
                top = f * step + i * blocks
                xs.append(rbuf[c, :, top:top + blocks, :].reshape(rows, LANES))
            if f == 1:
                gates = xs
            if f == 2:
                for i in range(per):
                    total = jnp.sum(jnp.sum(gates[i] * xs[i], axis=0, keepdims=True), axis=1, keepdims=True)
                    dsum[...] = jnp.where(spot == c * per + i, total, dsum[...])
            y = dot(first[...], split(jnp.concatenate(xs, axis=1), 0))
            for i in range(per):
                cut = slice(LANES * i, LANES * (i + 1))
                re, im = y[:rows, cut], y[rows:, cut]
                grown.append(jnp.concatenate([re * turn[0] - im * turn[1], re * turn[1] + im * turn[0]], axis=1))

        @pl.when(c == chunks - 1)
        def _():
            for k in range(1, n):
                summed(k).start()

        spec = dot(split(jnp.concatenate(grown, axis=0), 1), mid[...])
        prods = [[], [], []]
        for i in range(per):
            parts = []
            for f in range(3):
                top = (f * per + i) * rows
                parts.append((spec[top:top + rows, :LANES], spec[top:top + rows, LANES:]))
            (hr, hi), (gr, gi), (dr, di) = parts
            prods[0].append(jnp.concatenate([hr * gr - hi * gi, -(hr * gi + hi * gr)], axis=1))
            prods[1].append(jnp.concatenate([hr * dr + hi * di, hi * dr - hr * di], axis=1))
            prods[2].append(jnp.concatenate([gr * dr + gi * di, gi * dr - gr * di], axis=1))
        back = dot(split(jnp.concatenate(prods[0] + prods[1] + prods[2], axis=0), 1), mid[...])
        for f in range(3):
            cols = []
            for i in range(per):
                top = (f * per + i) * rows
                re, im = back[top:top + rows, :LANES], back[top:top + rows, LANES:]
                cols.append(jnp.concatenate([re * turn[0] - im * turn[1], re * turn[1] + im * turn[0]], axis=0))
            out = dot(last[...], split(jnp.concatenate(cols, axis=1), 0))
            for i in range(per):
                top = pl.multiple_of(lax.rem(c, join) * tall + f * step + i * blocks, blocks)
                obuf[c // join, :, pl.ds(top, blocks), :] = out[:, LANES * i:LANES * (i + 1)].reshape(n, blocks, LANES)

        @pl.when(lax.rem(c, join) == join - 1)
        def _():
            for k in range(1, n):
                outward(c // join, k).start()
            kept_out(c // join).start()

        return carry

    lax.fori_loop(0, chunks, chunk, 0)

    dgot[me] = dsum[...]
    for k in range(1, n):
        summed(k).wait()
    lane = lax.broadcasted_iota(jnp.int32, (chans, chans), 1)
    row = lax.broadcasted_iota(jnp.int32, (chans, chans), 0)
    gain = jnp.sum(jnp.where(lane == row, jnp.broadcast_to(skip[...], (chans, chans)), 0.0), axis=1, keepdims=True)
    for t in range(n):
        sums[t:t + 1, :] = dgot[t]
    found = sums[...]
    lane = lax.broadcasted_iota(jnp.int32, (n, chans), 1)
    row = lax.broadcasted_iota(jnp.int32, (n, chans), 0)
    line = jnp.zeros((n, chans), F32)
    for j in range(chunks * per):
        line = jnp.where(lane == j * n + row, found[:, j:j + 1], line)
    o_skip[...] = jnp.sum(line, axis=0, keepdims=True) * scale

    for c in range(chunks):
        down = slice(group * c, group * (c + 1))
        col = jnp.broadcast_to(gain[down], (group, LANES))
        if c % join == 0:
            for k in range(1, n):
                outward(c // join, k).wait()
            kept_out(c // join).wait()
        for q in range(blocks):
            at = (down, slice(LANES * q, LANES * (q + 1)))
            got = []
            for f in range(3):
                got.append(jnp.concatenate([gbuf[c // join, spread(f, i, q, c % join, join), :] for i in range(per)], axis=0))
            post_f, pre_f = post[at].astype(F32), pre[at].astype(F32)
            sig_f, cot_f = sig[at].astype(F32), cot[at].astype(F32)
            conved = got[0] + col * (pre_f * sig_f)
            o_out[at] = (post_f * conved).astype(BF16)
            o_post[at] = (cot_f * conved).astype(BF16)
            d_gated = got[1] + col * (cot_f * post_f)
            o_pre[at] = (d_gated * sig_f).astype(BF16)
            o_sig[at] = (d_gated * pre_f).astype(BF16)
            o_taps[at] = got[2] * scale


def store(*refs):
    half = len(refs) // 2
    for copy in fill(list(zip(refs[:half], refs[half:-1])), refs[-1]):
        copy.wait()


def solution(mesh):
    n = mesh.shape["seq"]
    chunks = 4
    join = 1

    def shards(post_gate, pre_gate, signal, cotangent, filter_taps, skip_gain):
        chans, length = filter_taps.shape
        blocks = length // LANES
        own = chans // n
        per = own // chunks
        first, mid, last, turn = tables(n * blocks, 2 * n * length)
        vmem = pl.BlockSpec(memory_space=pltpu.VMEM)
        hbm = pl.BlockSpec(memory_space=pltpu.HBM)
        half = jax.ShapeDtypeStruct((chans, length), BF16)
        results = (half, half, half, half, jax.ShapeDtypeStruct((1, chans), F32), jax.ShapeDtypeStruct((chans, length), F32))
        gates = pltpu.VMEM((chans, length), BF16)
        wide = pltpu.VMEM((chunks // join, n * 3 * per * blocks * join, LANES), F32)
        both = pltpu.VMEM((chunks // join, n, 3 * per * blocks * join, LANES), F32)
        few = pltpu.SemaphoreType.DMA((chunks // join, n))
        flat = pltpu.VMEM((chunks, n * 3 * per * blocks, LANES), F32)
        cut = pltpu.VMEM((chunks, n, 3 * per * blocks, LANES), F32)
        sem = pltpu.SemaphoreType.DMA((chunks, n))
        operands = (post_gate, pre_gate, signal, cotangent, filter_taps, first, mid, last, turn, skip_gain.reshape(1, chans))
        got = pl.pallas_call(
            functools.partial(exchange, n, chunks, join),
            out_shape=results,
            in_specs=[hbm] * 10,
            out_specs=[vmem] * 6,
            scratch_shapes=[
                gates, gates, gates, gates, pltpu.VMEM((chans, length), F32),
                pltpu.VMEM(first.shape, BF16), pltpu.VMEM(mid.shape, BF16), pltpu.VMEM(last.shape, BF16), pltpu.VMEM(turn.shape, F32),
                pltpu.VMEM((1, chans), F32),
                flat, cut, both, wide,
                pltpu.VMEM((1, LANES), F32), pltpu.VMEM((n, 1, LANES), F32), pltpu.VMEM((n, LANES), F32),
                pltpu.SemaphoreType.DMA((10,)),
                pltpu.SemaphoreType.DMA((2, chunks)), sem, sem, few, few,
                pltpu.SemaphoreType.DMA((n,)), pltpu.SemaphoreType.DMA((n,)),
            ],
            compiler_params=pltpu.CompilerParams(collective_id=0, has_side_effects=True, vmem_limit_bytes=32 << 20),
        )(*[pltpu.with_memory_space_constraint(x, pltpu.HBM) for x in operands])
        outs = pl.pallas_call(
            store,
            out_shape=results,
            in_specs=[vmem] * 6,
            out_specs=[hbm] * 6,
            scratch_shapes=[pltpu.SemaphoreType.DMA((6,))],
            compiler_params=pltpu.CompilerParams(vmem_limit_bytes=32 << 20),
        )(*got)
        return outs[0], outs[1], outs[2], outs[3], outs[4].reshape(chans), outs[5]

    return jax.shard_map(
        shards,
        mesh=mesh,
        in_specs=(P("chan", "seq"),) * 5 + (P("chan"),),
        out_specs=(P("chan", "seq"),) * 4 + (P("chan"), P("chan", "seq")),
        check_vma=False,
    )
```

```python
import functools
import math

import jax
import jax.numpy as jnp
import numpy as np
from jax import lax
from jax.experimental import pallas as pl
from jax.experimental.pallas import tpu as pltpu
from jax.sharding import PartitionSpec as P

LANES = 128
SUB = 8
F32 = jnp.float32
BF16 = jnp.bfloat16


def halves(table):
    high = table.astype(jnp.bfloat16)
    low = (table - high.astype(np.float64)).astype(jnp.bfloat16)
    return high, low


def tables(rows, padded):
    a = np.arange(rows)[:, None]
    b = np.arange(rows)[None, :] + 0.5
    theta = 2.0 * math.pi * a * b / (2 * rows)
    first = np.concatenate([np.cos(theta).T, -np.sin(theta).T], axis=0)
    last = np.concatenate([np.cos(theta), np.sin(theta)], axis=1) * (2.0 / padded)
    r = np.arange(LANES)
    phi = 2.0 * math.pi * (np.arange(rows)[:, None] + 0.5) * r[None, :] / padded
    turn = np.stack([np.cos(phi), -np.sin(phi)]).astype(np.float32)
    psi = 2.0 * math.pi * np.outer(r, r) / LANES
    cos_m, sin_m = np.cos(psi), np.sin(psi)
    mid = np.block([[cos_m, -sin_m], [sin_m, cos_m]])
    f_hi, f_lo = halves(first)
    m_hi, m_lo = halves(mid)
    l_hi, l_lo = halves(last)
    return (
        np.concatenate([f_hi, f_hi, f_lo], axis=1),
        np.concatenate([m_hi, m_hi, m_lo], axis=0),
        np.concatenate([l_hi, l_hi, l_lo], axis=1),
        turn,
    )


def split(value, axis):
    high = value.astype(BF16)
    low = (value - high.astype(F32)).astype(BF16)
    return jnp.concatenate([high, low, high], axis=axis)


def dot(left, right):
    return jnp.dot(left, right, preferred_element_type=F32)


def fill(pairs, sems):
    copies = [pltpu.make_async_copy(src, dst, sems.at[i]) for i, (src, dst) in enumerate(pairs)]
    for copy in copies:
        copy.start()
    return copies


def weigh(c, n, per, down, to, col, gbuf, post, pre, sig, cot, o_out, o_post, o_pre, o_sig, o_taps):
    blocks = post.shape[1] // LANES
    step = per * blocks
    scale = 1.0 / math.sqrt(n * post.shape[1])
    for q in range(blocks):
        side = slice(LANES * q, LANES * (q + 1))
        at, put = (down, side), (to, side)
        got = []
        for f in range(3):
            got.append(jnp.concatenate(
                [gbuf[c, pl.ds(f * step + i * blocks + q, n, stride=3 * step), :] for i in range(per)], axis=0))
        post_f, pre_f = post[at].astype(F32), pre[at].astype(F32)
        sig_f, cot_f = sig[at].astype(F32), cot[at].astype(F32)
        conved = got[0] + col * (pre_f * sig_f)
        o_out[put] = (post_f * conved).astype(BF16)
        o_post[put] = (cot_f * conved).astype(BF16)
        d_gated = got[1] + col * (cot_f * post_f)
        o_pre[put] = (d_gated * sig_f).astype(BF16)
        o_sig[put] = (d_gated * pre_f).astype(BF16)
        o_taps[put] = got[2] * scale


def exchange(
    n, chunks, join,
    h_post, h_pre, h_sig, h_cot, h_taps, h_first, h_mid, h_last, h_turn, h_skip,
    o_out, o_post, o_pre, o_sig, o_skip, o_taps, gbuf, post, pre, sig, cot, wide_gain,
    taps, first, mid, last, turn, skip, sbuf, rbuf, obuf, dsum, dgot, sums,
    load_sem, self_sem, s_in, r_in, s_out, r_out, s_sum, r_sum,
):
    me = lax.axis_index("seq")
    chans, length = taps.shape
    blocks = length // LANES
    rows = n * blocks
    group = chans // chunks
    per = group // n
    step = per * blocks
    tall = 3 * step
    scale = 1.0 / math.sqrt(n * length)

    barrier = pltpu.get_barrier_semaphore()
    for k in range(1, n):
        pl.semaphore_signal(barrier, inc=1, device_id={"seq": lax.rem(me + k, n)})
    loads = fill(
        [(h_taps, taps), (h_pre, pre), (h_sig, sig), (h_cot, cot), (h_post, post),
         (h_first, first), (h_mid, mid), (h_turn, turn), (h_last, last), (h_skip, skip)], load_sem)
    for load in loads[:5]:
        load.wait()

    def peer(k):
        return lax.rem(me + k, n)

    def wide_of(t):
        return pl.ds(pl.multiple_of(t * join * tall, join * tall), join * tall)

    def rows_of(t):
        return pl.ds(pl.multiple_of(t * tall, tall), tall)

    def spread(f, i, q, more=0, wide=1):
        return pl.ds(more * tall + f * step + i * blocks + q, n, stride=wide * tall)

    def inward(c, k):
        return pltpu.make_async_remote_copy(
            src_ref=sbuf.at[c, rows_of(peer(k))], dst_ref=rbuf.at[c, me],
            send_sem=s_in.at[c, k], recv_sem=r_in.at[c, k], device_id={"seq": peer(k)},
        )

    def outward(c, k):
        return pltpu.make_async_remote_copy(
            src_ref=obuf.at[c, peer(k)], dst_ref=gbuf.at[c, wide_of(me)],
            send_sem=s_out.at[c, k], recv_sem=r_out.at[c, k], device_id={"seq": peer(k)},
        )

    def summed(k):
        return pltpu.make_async_remote_copy(
            src_ref=dsum, dst_ref=dgot.at[me],
            send_sem=s_sum.at[k], recv_sem=r_sum.at[k], device_id={"seq": peer(k)},
        )

    def kept_in(c):
        return pltpu.make_async_copy(sbuf.at[c, rows_of(me)], rbuf.at[c, me], self_sem.at[0, c])

    def kept_out(c):
        return pltpu.make_async_copy(obuf.at[c, me], gbuf.at[c, wide_of(me)], self_sem.at[1, c])

    for c in range(chunks):
        for q in range(blocks):
            at = (slice(group * c, group * (c + 1)), slice(LANES * q, LANES * (q + 1)))
            gated = pre[at].astype(F32) * sig[at].astype(F32)
            slope = cot[at].astype(F32) * post[at].astype(F32)
            for f, value in enumerate((taps[at], gated, slope)):
                for i in range(per):
                    sbuf[c, spread(f, i, q), :] = value[n * i:n * (i + 1)]
        if c == 0:
            pl.semaphore_wait(barrier, n - 1)
        for k in range(1, n):
            inward(c, k).start()
        kept_in(c).start()
    for load in loads[5:]:
        load.wait()

    spot = lax.broadcasted_iota(jnp.int32, (1, LANES), 1)
    dsum[...] = jnp.zeros_like(dsum)

    def chunk(c, carry):
        for k in range(1, n):
            inward(c, k).wait()
        kept_in(c).wait()
        grown = []
        gates = []
        for f in range(3):
            xs = []
            for i in range(per):
                top = f * step + i * blocks
                xs.append(rbuf[c, :, top:top + blocks, :].reshape(rows, LANES))
            if f == 1:
                gates = xs
            if f == 2:
                for i in range(per):
                    total = jnp.sum(jnp.sum(gates[i] * xs[i], axis=0, keepdims=True), axis=1, keepdims=True)
                    dsum[...] = jnp.where(spot == c * per + i, total, dsum[...])
            y = dot(first[...], split(jnp.concatenate(xs, axis=1), 0))
            for i in range(per):
                cut = slice(LANES * i, LANES * (i + 1))
                re, im = y[:rows, cut], y[rows:, cut]
                grown.append(jnp.concatenate([re * turn[0] - im * turn[1], re * turn[1] + im * turn[0]], axis=1))

        @pl.when(c == chunks - 1)
        def _():
            for k in range(1, n):
                summed(k).start()

        spec = dot(split(jnp.concatenate(grown, axis=0), 1), mid[...])
        prods = [[], [], []]
        for i in range(per):
            parts = []
            for f in range(3):
                top = (f * per + i) * rows
                parts.append((spec[top:top + rows, :LANES], spec[top:top + rows, LANES:]))
            (hr, hi), (gr, gi), (dr, di) = parts
            prods[0].append(jnp.concatenate([hr * gr - hi * gi, -(hr * gi + hi * gr)], axis=1))
            prods[1].append(jnp.concatenate([hr * dr + hi * di, hi * dr - hr * di], axis=1))
            prods[2].append(jnp.concatenate([gr * dr + gi * di, gi * dr - gr * di], axis=1))
        back = dot(split(jnp.concatenate(prods[0] + prods[1] + prods[2], axis=0), 1), mid[...])
        for f in range(3):
            cols = []
            for i in range(per):
                top = (f * per + i) * rows
                re, im = back[top:top + rows, :LANES], back[top:top + rows, LANES:]
                cols.append(jnp.concatenate([re * turn[0] - im * turn[1], re * turn[1] + im * turn[0]], axis=0))
            out = dot(last[...], split(jnp.concatenate(cols, axis=1), 0))
            for i in range(per):
                top = pl.multiple_of(lax.rem(c, join) * tall + f * step + i * blocks, blocks)
                obuf[c // join, :, pl.ds(top, blocks), :] = out[:, LANES * i:LANES * (i + 1)].reshape(n, blocks, LANES)

        @pl.when(lax.rem(c, join) == join - 1)
        def _():
            for k in range(1, n):
                outward(c // join, k).start()
            kept_out(c // join).start()

        return carry

    lax.fori_loop(0, chunks, chunk, 0)

    dgot[me] = dsum[...]
    for k in range(1, n):
        summed(k).wait()
    lane = lax.broadcasted_iota(jnp.int32, (chans, chans), 1)
    row = lax.broadcasted_iota(jnp.int32, (chans, chans), 0)
    gain = jnp.sum(jnp.where(lane == row, jnp.broadcast_to(skip[...], (chans, chans)), 0.0), axis=1, keepdims=True)
    for t in range(n):
        sums[t:t + 1, :] = dgot[t]
    found = sums[...]
    lane = lax.broadcasted_iota(jnp.int32, (n, chans), 1)
    row = lax.broadcasted_iota(jnp.int32, (n, chans), 0)
    line = jnp.zeros((n, chans), F32)
    for j in range(chunks * per):
        line = jnp.where(lane == j * n + row, found[:, j:j + 1], line)
    o_skip[...] = jnp.sum(line, axis=0, keepdims=True) * scale

    for c in range(chunks):
        down = slice(group * c, group * (c + 1))
        col = jnp.broadcast_to(gain[down], (group, LANES))
        if c % join == 0:
            for k in range(1, n):
                outward(c // join, k).wait()
            kept_out(c // join).wait()
        if c < chunks - 1:
            weigh(c, n, per, down, down, col, gbuf, post, pre, sig, cot, o_out, o_post, o_pre, o_sig, o_taps)
    wide_gain[...] = jnp.broadcast_to(gain[group * (chunks - 1):], wide_gain.shape)


def store(n, per, r_out, r_post, r_pre, r_sig, r_skip, r_taps, gbuf, post, pre, sig, cot, wide_gain,
          h_out, h_post, h_pre, h_sig, h_skip, h_taps, l_out, l_post, l_pre, l_sig, l_taps, sems):
    chans = post.shape[0]
    group = n * per
    head, tail = slice(0, chans - group), slice(chans - group, chans)
    ends = (h_out, h_post, h_pre, h_sig, h_taps)
    copies = fill([(src.at[head], dst.at[head]) for src, dst in zip((r_out, r_post, r_pre, r_sig, r_taps), ends)]
                  + [(r_skip, h_skip)], sems.at[0])
    rest = (l_out, l_post, l_pre, l_sig, l_taps)
    weigh(gbuf.shape[0] - 1, n, per, tail, slice(0, group), wide_gain[...], gbuf, post, pre, sig, cot, *rest)
    copies += fill([(src, dst.at[tail]) for src, dst in zip(rest, ends)], sems.at[1])
    for copy in copies:
        copy.wait()


def solution(mesh):
    n = mesh.shape["seq"]
    chunks = 4
    join = 1

    def shards(post_gate, pre_gate, signal, cotangent, filter_taps, skip_gain):
        chans, length = filter_taps.shape
        blocks = length // LANES
        own = chans // n
        per = own // chunks
        first, mid, last, turn = tables(n * blocks, 2 * n * length)
        vmem = pl.BlockSpec(memory_space=pltpu.VMEM)
        hbm = pl.BlockSpec(memory_space=pltpu.HBM)
        half = jax.ShapeDtypeStruct((chans, length), BF16)
        results = (half, half, half, half, jax.ShapeDtypeStruct((1, chans), F32), jax.ShapeDtypeStruct((chans, length), F32))
        carried = (jax.ShapeDtypeStruct((chunks // join, n * 3 * per * blocks * join, LANES), F32),
                   half, half, half, half, jax.ShapeDtypeStruct((n * per, LANES), F32))
        both = pltpu.VMEM((chunks // join, n, 3 * per * blocks * join, LANES), F32)
        few = pltpu.SemaphoreType.DMA((chunks // join, n))
        flat = pltpu.VMEM((chunks, n * 3 * per * blocks, LANES), F32)
        cut = pltpu.VMEM((chunks, n, 3 * per * blocks, LANES), F32)
        sem = pltpu.SemaphoreType.DMA((chunks, n))
        operands = (post_gate, pre_gate, signal, cotangent, filter_taps, first, mid, last, turn, skip_gain.reshape(1, chans))
        got = pl.pallas_call(
            functools.partial(exchange, n, chunks, join),
            out_shape=results + carried,
            in_specs=[hbm] * 10,
            out_specs=[vmem] * 12,
            scratch_shapes=[
                pltpu.VMEM((chans, length), F32),
                pltpu.VMEM(first.shape, BF16), pltpu.VMEM(mid.shape, BF16), pltpu.VMEM(last.shape, BF16), pltpu.VMEM(turn.shape, F32),
                pltpu.VMEM((1, chans), F32),
                flat, cut, both,
                pltpu.VMEM((1, LANES), F32), pltpu.VMEM((n, 1, LANES), F32), pltpu.VMEM((n, LANES), F32),
                pltpu.SemaphoreType.DMA((10,)),
                pltpu.SemaphoreType.DMA((2, chunks)), sem, sem, few, few,
                pltpu.SemaphoreType.DMA((n,)), pltpu.SemaphoreType.DMA((n,)),
            ],
            compiler_params=pltpu.CompilerParams(collective_id=0, has_side_effects=True, vmem_limit_bytes=32 << 20),
        )(*[pltpu.with_memory_space_constraint(x, pltpu.HBM) for x in operands])
        outs = pl.pallas_call(
            functools.partial(store, n, per),
            out_shape=results,
            in_specs=[vmem] * 12,
            out_specs=[hbm] * 6,
            scratch_shapes=[pltpu.VMEM((n * per, length), BF16)] * 4 + [
                pltpu.VMEM((n * per, length), F32), pltpu.SemaphoreType.DMA((2, 6))],
            compiler_params=pltpu.CompilerParams(vmem_limit_bytes=32 << 20),
        )(*got)
        return outs[0], outs[1], outs[2], outs[3], outs[4].reshape(chans), outs[5]

    return jax.shard_map(
        shards,
        mesh=mesh,
        in_specs=(P("chan", "seq"),) * 5 + (P("chan"),),
        out_specs=(P("chan", "seq"),) * 4 + (P("chan"), P("chan", "seq")),
        check_vma=False,
    )
```

```python
import functools
import math

import jax
import jax.numpy as jnp
import numpy as np
from jax import lax
from jax.experimental import pallas as pl
from jax.experimental.pallas import tpu as pltpu
from jax.sharding import PartitionSpec as P

LANES = 128
SUB = 8
F32 = jnp.float32
BF16 = jnp.bfloat16


def halves(table):
    high = table.astype(jnp.bfloat16)
    low = (table - high.astype(np.float64)).astype(jnp.bfloat16)
    return high, low


def tables(rows, padded):
    a = np.arange(rows)[:, None]
    b = np.arange(rows)[None, :] + 0.5
    theta = 2.0 * math.pi * a * b / (2 * rows)
    first = np.concatenate([np.cos(theta).T, -np.sin(theta).T], axis=0)
    last = np.concatenate([np.cos(theta), np.sin(theta)], axis=1) * (2.0 / padded)
    r = np.arange(LANES)
    phi = 2.0 * math.pi * (np.arange(rows)[:, None] + 0.5) * r[None, :] / padded
    turn = np.stack([np.cos(phi), -np.sin(phi)]).astype(np.float32)
    psi = 2.0 * math.pi * np.outer(r, r) / LANES
    cos_m, sin_m = np.cos(psi), np.sin(psi)
    mid = np.block([[cos_m, -sin_m], [sin_m, cos_m]])
    f_hi, f_lo = halves(first)
    m_hi, m_lo = halves(mid)
    l_hi, l_lo = halves(last)
    return (
        np.concatenate([f_hi, f_hi, f_lo], axis=1),
        np.concatenate([m_hi, m_hi, m_lo], axis=0),
        np.concatenate([l_hi, l_hi, l_lo], axis=1),
        turn,
    )


def split(value, axis):
    high = value.astype(BF16)
    low = (value - high.astype(F32)).astype(BF16)
    return jnp.concatenate([high, low, high], axis=axis)


def dot(left, right):
    return jnp.dot(left, right, preferred_element_type=F32)


def fill(pairs, sems):
    copies = [pltpu.make_async_copy(src, dst, sems.at[i]) for i, (src, dst) in enumerate(pairs)]
    for copy in copies:
        copy.start()
    return copies


def exchange(
    n, chunks, join,
    h_post, h_pre, h_sig, h_cot, h_taps, h_first, h_mid, h_last, h_turn, h_skip,
    o_out, o_post, o_pre, o_sig, o_skip, o_taps,
    post, pre, sig, cot, taps, first, mid, last, turn, skip, sbuf, rbuf, obuf, gbuf, dsum, dgot, sums, gains,
    load_sem, self_sem, s_in, r_in, s_out, r_out, s_sum, r_sum,
):
    me = lax.axis_index("seq")
    chans, length = taps.shape
    blocks = length // LANES
    rows = n * blocks
    group = chans // chunks
    per = group // n
    step = per * blocks
    tall = 3 * step
    scale = 1.0 / math.sqrt(n * length)

    barrier = pltpu.get_barrier_semaphore()
    for k in range(1, n):
        pl.semaphore_signal(barrier, inc=1, device_id={"seq": lax.rem(me + k, n)})
    loads = fill(
        [(h_taps, taps), (h_pre, pre), (h_sig, sig), (h_cot, cot), (h_post, post),
         (h_first, first), (h_mid, mid), (h_turn, turn), (h_last, last), (h_skip, skip)], load_sem)
    for load in loads[:5]:
        load.wait()

    def peer(k):
        return lax.rem(me + k, n)

    def wide_of(t):
        return pl.ds(pl.multiple_of(t * join * tall, join * tall), join * tall)

    def rows_of(t):
        return pl.ds(pl.multiple_of(t * tall, tall), tall)

    def spread(f, i, q, more=0, wide=1):
        return pl.ds(more * tall + f * step + i * blocks + q, n, stride=wide * tall)

    def inward(c, k):
        return pltpu.make_async_remote_copy(
            src_ref=sbuf.at[c, rows_of(peer(k))], dst_ref=rbuf.at[c, me],
            send_sem=s_in.at[c, k], recv_sem=r_in.at[c, k], device_id={"seq": peer(k)},
        )

    def outward(c, k):
        return pltpu.make_async_remote_copy(
            src_ref=obuf.at[c, peer(k)], dst_ref=gbuf.at[c, wide_of(me)],
            send_sem=s_out.at[c, k], recv_sem=r_out.at[c, k], device_id={"seq": peer(k)},
        )

    def summed(k):
        return pltpu.make_async_remote_copy(
            src_ref=dsum, dst_ref=dgot.at[me],
            send_sem=s_sum.at[k], recv_sem=r_sum.at[k], device_id={"seq": peer(k)},
        )

    def kept_in(c):
        return pltpu.make_async_copy(sbuf.at[c, rows_of(me)], rbuf.at[c, me], self_sem.at[0, c])

    def kept_out(c):
        return pltpu.make_async_copy(obuf.at[c, me], gbuf.at[c, wide_of(me)], self_sem.at[1, c])

    for c in range(chunks):
        for q in range(blocks):
            at = (slice(group * c, group * (c + 1)), slice(LANES * q, LANES * (q + 1)))
            gated = pre[at].astype(F32) * sig[at].astype(F32)
            slope = cot[at].astype(F32) * post[at].astype(F32)
            for f, value in enumerate((taps[at], gated, slope)):
                for i in range(per):
                    sbuf[c, spread(f, i, q), :] = value[n * i:n * (i + 1)]
        if c == 0:
            pl.semaphore_wait(barrier, n - 1)
        for k in range(1, n):
            inward(c, k).start()
        kept_in(c).start()
    for load in loads[5:]:
        load.wait()

    spot = lax.broadcasted_iota(jnp.int32, (1, LANES), 1)
    dsum[...] = jnp.zeros_like(dsum)

    def chunk(c, carry):
        for k in range(1, n):
            inward(c, k).wait()
        kept_in(c).wait()
        grown = []
        gates = []
        for f in range(3):
            xs = []
            for i in range(per):
                top = f * step + i * blocks
                xs.append(rbuf[c, :, top:top + blocks, :].reshape(rows, LANES))
            if f == 1:
                gates = xs
            if f == 2:
                for i in range(per):
                    total = jnp.sum(jnp.sum(gates[i] * xs[i], axis=0, keepdims=True), axis=1, keepdims=True)
                    dsum[...] = jnp.where(spot == c * per + i, total, dsum[...])
            y = dot(first[...], split(jnp.concatenate(xs, axis=1), 0))
            for i in range(per):
                cut = slice(LANES * i, LANES * (i + 1))
                re, im = y[:rows, cut], y[rows:, cut]
                grown.append(jnp.concatenate([re * turn[0] - im * turn[1], re * turn[1] + im * turn[0]], axis=1))

        @pl.when(c == chunks - 1)
        def _():
            for k in range(1, n):
                summed(k).start()

        spec = dot(split(jnp.concatenate(grown, axis=0), 1), mid[...])
        prods = [[], [], []]
        for i in range(per):
            parts = []
            for f in range(3):
                top = (f * per + i) * rows
                parts.append((spec[top:top + rows, :LANES], spec[top:top + rows, LANES:]))
            (hr, hi), (gr, gi), (dr, di) = parts
            prods[0].append(jnp.concatenate([hr * gr - hi * gi, -(hr * gi + hi * gr)], axis=1))
            prods[1].append(jnp.concatenate([hr * dr + hi * di, hi * dr - hr * di], axis=1))
            prods[2].append(jnp.concatenate([gr * dr + gi * di, gi * dr - gr * di], axis=1))
        back = dot(split(jnp.concatenate(prods[0] + prods[1] + prods[2], axis=0), 1), mid[...])
        for f in range(3):
            cols = []
            for i in range(per):
                top = (f * per + i) * rows
                re, im = back[top:top + rows, :LANES], back[top:top + rows, LANES:]
                cols.append(jnp.concatenate([re * turn[0] - im * turn[1], re * turn[1] + im * turn[0]], axis=0))
            out = dot(last[...], split(jnp.concatenate(cols, axis=1), 0))
            for i in range(per):
                top = pl.multiple_of(lax.rem(c, join) * tall + f * step + i * blocks, blocks)
                obuf[c // join, :, pl.ds(top, blocks), :] = out[:, LANES * i:LANES * (i + 1)].reshape(n, blocks, LANES)

        @pl.when(lax.rem(c, join) == join - 1)
        def _():
            for k in range(1, n):
                outward(c // join, k).start()
            kept_out(c // join).start()

        return carry

    lax.fori_loop(0, chunks, chunk, 0)

    dgot[me] = dsum[...]
    for k in range(1, n):
        summed(k).wait()
    lane = lax.broadcasted_iota(jnp.int32, (chans, chans), 1)
    row = lax.broadcasted_iota(jnp.int32, (chans, chans), 0)
    gain = jnp.sum(jnp.where(lane == row, jnp.broadcast_to(skip[...], (chans, chans)), 0.0), axis=1, keepdims=True)
    for t in range(n):
        sums[t:t + 1, :] = dgot[t]
    found = sums[...]
    lane = lax.broadcasted_iota(jnp.int32, (n, chans), 1)
    row = lax.broadcasted_iota(jnp.int32, (n, chans), 0)
    line = jnp.zeros((n, chans), F32)
    for j in range(chunks * per):
        line = jnp.where(lane == j * n + row, found[:, j:j + 1], line)
    o_skip[...] = jnp.sum(line, axis=0, keepdims=True) * scale

    gains[...] = jnp.broadcast_to(gain, gains.shape)

    def settle(c, carry):
        down = pl.ds(pl.multiple_of(c * group, group), group)
        col = gains[down, :]
        for k in range(1, n):
            outward(c, k).wait()
        kept_out(c).wait()
        for q in range(blocks):
            at = (down, slice(LANES * q, LANES * (q + 1)))
            got = []
            for f in range(3):
                got.append(jnp.concatenate([gbuf[c, spread(f, i, q), :] for i in range(per)], axis=0))
            post_f, pre_f = post[at].astype(F32), pre[at].astype(F32)
            sig_f, cot_f = sig[at].astype(F32), cot[at].astype(F32)
            conved = got[0] + col * (pre_f * sig_f)
            o_out[at] = (post_f * conved).astype(BF16)
            o_post[at] = (cot_f * conved).astype(BF16)
            d_gated = got[1] + col * (cot_f * post_f)
            o_pre[at] = (d_gated * sig_f).astype(BF16)
            o_sig[at] = (d_gated * pre_f).astype(BF16)
            o_taps[at] = got[2] * scale
        return carry

    lax.fori_loop(0, chunks, settle, 0)


def store(*refs):
    half = len(refs) // 2
    for copy in fill(list(zip(refs[:half], refs[half:-1])), refs[-1]):
        copy.wait()


def solution(mesh):
    n = mesh.shape["seq"]
    chunks = 4
    join = 1

    def shards(post_gate, pre_gate, signal, cotangent, filter_taps, skip_gain):
        chans, length = filter_taps.shape
        blocks = length // LANES
        own = chans // n
        per = own // chunks
        first, mid, last, turn = tables(n * blocks, 2 * n * length)
        vmem = pl.BlockSpec(memory_space=pltpu.VMEM)
        hbm = pl.BlockSpec(memory_space=pltpu.HBM)
        half = jax.ShapeDtypeStruct((chans, length), BF16)
        results = (half, half, half, half, jax.ShapeDtypeStruct((1, chans), F32), jax.ShapeDtypeStruct((chans, length), F32))
        gates = pltpu.VMEM((chans, length), BF16)
        wide = pltpu.VMEM((chunks // join, n * 3 * per * blocks * join, LANES), F32)
        both = pltpu.VMEM((chunks // join, n, 3 * per * blocks * join, LANES), F32)
        few = pltpu.SemaphoreType.DMA((chunks // join, n))
        flat = pltpu.VMEM((chunks, n * 3 * per * blocks, LANES), F32)
        cut = pltpu.VMEM((chunks, n, 3 * per * blocks, LANES), F32)
        sem = pltpu.SemaphoreType.DMA((chunks, n))
        operands = (post_gate, pre_gate, signal, cotangent, filter_taps, first, mid, last, turn, skip_gain.reshape(1, chans))
        got = pl.pallas_call(
            functools.partial(exchange, n, chunks, join),
            out_shape=results,
            in_specs=[hbm] * 10,
            out_specs=[vmem] * 6,
            scratch_shapes=[
                gates, gates, gates, gates, pltpu.VMEM((chans, length), F32),
                pltpu.VMEM(first.shape, BF16), pltpu.VMEM(mid.shape, BF16), pltpu.VMEM(last.shape, BF16), pltpu.VMEM(turn.shape, F32),
                pltpu.VMEM((1, chans), F32),
                flat, cut, both, wide,
                pltpu.VMEM((1, LANES), F32), pltpu.VMEM((n, 1, LANES), F32), pltpu.VMEM((n, LANES), F32),
                pltpu.VMEM((chans, LANES), F32),
                pltpu.SemaphoreType.DMA((10,)),
                pltpu.SemaphoreType.DMA((2, chunks)), sem, sem, few, few,
                pltpu.SemaphoreType.DMA((n,)), pltpu.SemaphoreType.DMA((n,)),
            ],
            compiler_params=pltpu.CompilerParams(collective_id=0, has_side_effects=True, vmem_limit_bytes=32 << 20),
        )(*[pltpu.with_memory_space_constraint(x, pltpu.HBM) for x in operands])
        outs = pl.pallas_call(
            store,
            out_shape=results,
            in_specs=[vmem] * 6,
            out_specs=[hbm] * 6,
            scratch_shapes=[pltpu.SemaphoreType.DMA((6,))],
            compiler_params=pltpu.CompilerParams(vmem_limit_bytes=32 << 20),
        )(*got)
        return outs[0], outs[1], outs[2], outs[3], outs[4].reshape(chans), outs[5]

    return jax.shard_map(
        shards,
        mesh=mesh,
        in_specs=(P("chan", "seq"),) * 5 + (P("chan"),),
        out_specs=(P("chan", "seq"),) * 4 + (P("chan"), P("chan", "seq")),
        check_vma=False,
    )
```

```python
import functools
import math

import jax
import jax.numpy as jnp
import numpy as np
from jax import lax
from jax.experimental import pallas as pl
from jax.experimental.pallas import tpu as pltpu
from jax.sharding import PartitionSpec as P

LANES = 128
SUB = 8
F32 = jnp.float32
BF16 = jnp.bfloat16


def halves(table):
    high = table.astype(jnp.bfloat16)
    low = (table - high.astype(np.float64)).astype(jnp.bfloat16)
    return high, low


def tables(rows, padded):
    a = np.arange(rows)[:, None]
    b = np.arange(rows)[None, :] + 0.5
    theta = 2.0 * math.pi * a * b / (2 * rows)
    first = np.concatenate([np.cos(theta).T, -np.sin(theta).T], axis=0)
    last = np.concatenate([np.cos(theta), np.sin(theta)], axis=1) * (2.0 / padded)
    r = np.arange(LANES)
    phi = 2.0 * math.pi * (np.arange(rows)[:, None] + 0.5) * r[None, :] / padded
    turn = np.stack([np.cos(phi), -np.sin(phi)]).astype(np.float32)
    psi = 2.0 * math.pi * np.outer(r, r) / LANES
    cos_m, sin_m = np.cos(psi), np.sin(psi)
    mid = np.block([[cos_m, -sin_m], [sin_m, cos_m]])
    f_hi, f_lo = halves(first)
    m_hi, m_lo = halves(mid)
    l_hi, l_lo = halves(last)
    return (
        np.concatenate([f_hi, f_hi, f_lo], axis=1),
        np.concatenate([m_hi, m_hi, m_lo], axis=0),
        np.concatenate([l_hi, l_hi, l_lo], axis=1),
        turn,
    )


def split(value, axis):
    high = value.astype(BF16)
    low = (value - high.astype(F32)).astype(BF16)
    return jnp.concatenate([high, low, high], axis=axis)


def dot(left, right):
    return jnp.dot(left, right, preferred_element_type=F32)


def fill(pairs, sems):
    copies = [pltpu.make_async_copy(src, dst, sems.at[i]) for i, (src, dst) in enumerate(pairs)]
    for copy in copies:
        copy.start()
    return copies


def exchange(
    n, chunks, join,
    h_post, h_pre, h_sig, h_cot, h_taps, h_first, h_mid, h_last, h_turn, h_skip,
    o_out, o_post, o_pre, o_sig, o_skip, o_taps,
    post, pre, sig, cot, taps, first, mid, last, turn, skip, sbuf, rbuf, obuf, gbuf, dsum, dgot, sums,
    load_sem, self_sem, s_in, r_in, s_out, r_out, s_sum, r_sum,
):
    me = lax.axis_index("seq")
    chans, length = taps.shape
    blocks = length // LANES
    rows = n * blocks
    group = chans // chunks
    per = group // n
    step = per * blocks
    tall = 3 * step
    scale = 1.0 / math.sqrt(n * length)

    barrier = pltpu.get_barrier_semaphore()
    for k in range(1, n):
        pl.semaphore_signal(barrier, inc=1, device_id={"seq": lax.rem(me + k, n)})
    loads = fill(
        [(h_taps, taps), (h_pre, pre), (h_sig, sig), (h_cot, cot), (h_post, post),
         (h_first, first), (h_mid, mid), (h_turn, turn), (h_last, last), (h_skip, skip)], load_sem)
    for load in loads[:5]:
        load.wait()

    def peer(k):
        return lax.rem(me + k, n)

    def wide_of(t):
        return pl.ds(pl.multiple_of(t * join * tall, join * tall), join * tall)

    def rows_of(t):
        return pl.ds(pl.multiple_of(t * tall, tall), tall)

    def spread(f, i, q, more=0, wide=1):
        return pl.ds(more * tall + f * step + i * blocks + q, n, stride=wide * tall)

    def inward(c, k):
        return pltpu.make_async_remote_copy(
            src_ref=sbuf.at[c, rows_of(peer(k))], dst_ref=rbuf.at[c, me],
            send_sem=s_in.at[c, k], recv_sem=r_in.at[c, k], device_id={"seq": peer(k)},
        )

    def outward(c, k):
        return pltpu.make_async_remote_copy(
            src_ref=obuf.at[c, peer(k)], dst_ref=gbuf.at[c, wide_of(me)],
            send_sem=s_out.at[c, k], recv_sem=r_out.at[c, k], device_id={"seq": peer(k)},
        )

    def summed(k):
        return pltpu.make_async_remote_copy(
            src_ref=dsum, dst_ref=dgot.at[me],
            send_sem=s_sum.at[k], recv_sem=r_sum.at[k], device_id={"seq": peer(k)},
        )

    def kept_in(c):
        return pltpu.make_async_copy(sbuf.at[c, rows_of(me)], rbuf.at[c, me], self_sem.at[0, c])

    def kept_out(c):
        return pltpu.make_async_copy(obuf.at[c, me], gbuf.at[c, wide_of(me)], self_sem.at[1, c])

    for c in range(chunks):
        for q in range(blocks):
            at = (slice(group * c, group * (c + 1)), slice(LANES * q, LANES * (q + 1)))
            gated = pre[at].astype(F32) * sig[at].astype(F32)
            slope = cot[at].astype(F32) * post[at].astype(F32)
            for f, value in enumerate((taps[at], gated, slope)):
                for i in range(per):
                    sbuf[c, spread(f, i, q), :] = value[n * i:n * (i + 1)]
        if c == 0:
            pl.semaphore_wait(barrier, n - 1)
        for k in range(1, n):
            inward(c, k).start()
        kept_in(c).start()
    for load in loads[5:]:
        load.wait()

    spot = lax.broadcasted_iota(jnp.int32, (1, LANES), 1)
    dsum[...] = jnp.zeros_like(dsum)

    def chunk(c, carry):
        for k in range(1, n):
            inward(c, k).wait()
        kept_in(c).wait()
        grown = []
        gates = []
        for f in range(3):
            xs = []
            for i in range(per):
                top = f * step + i * blocks
                xs.append(rbuf[c, :, top:top + blocks, :].reshape(rows, LANES))
            if f == 1:
                gates = xs
            if f == 2:
                for i in range(per):
                    total = jnp.sum(jnp.sum(gates[i] * xs[i], axis=0, keepdims=True), axis=1, keepdims=True)
                    dsum[...] = jnp.where(spot == c * per + i, total, dsum[...])
            y = dot(first[...], split(jnp.concatenate(xs, axis=1), 0))
            for i in range(per):
                cut = slice(LANES * i, LANES * (i + 1))
                re, im = y[:rows, cut], y[rows:, cut]
                grown.append(jnp.concatenate([re * turn[0] - im * turn[1], re * turn[1] + im * turn[0]], axis=1))

        @pl.when(c == chunks - 1)
        def _():
            for k in range(1, n):
                summed(k).start()

        spec = dot(split(jnp.concatenate(grown, axis=0), 1), mid[...])
        prods = [[], [], []]
        for i in range(per):
            parts = []
            for f in range(3):
                top = (f * per + i) * rows
                parts.append((spec[top:top + rows, :LANES], spec[top:top + rows, LANES:]))
            (hr, hi), (gr, gi), (dr, di) = parts
            prods[0].append(jnp.concatenate([hr * gr - hi * gi, -(hr * gi + hi * gr)], axis=1))
            prods[1].append(jnp.concatenate([hr * dr + hi * di, hi * dr - hr * di], axis=1))
            prods[2].append(jnp.concatenate([gr * dr + gi * di, gi * dr - gr * di], axis=1))
        back = dot(split(jnp.concatenate(prods[0] + prods[1] + prods[2], axis=0), 1), mid[...])
        for f in range(3):
            cols = []
            for i in range(per):
                top = (f * per + i) * rows
                re, im = back[top:top + rows, :LANES], back[top:top + rows, LANES:]
                cols.append(jnp.concatenate([re * turn[0] - im * turn[1], re * turn[1] + im * turn[0]], axis=0))
            out = dot(last[...], split(jnp.concatenate(cols, axis=1), 0))
            for i in range(per):
                top = pl.multiple_of(lax.rem(c, join) * tall + f * step + i * blocks, blocks)
                obuf[c // join, :, pl.ds(top, blocks), :] = out[:, LANES * i:LANES * (i + 1)].reshape(n, blocks, LANES)

        @pl.when(lax.rem(c, join) == join - 1)
        def _():
            for k in (2, 6, 3, 5, 1, 7, 4):
                outward(c // join, k).start()
            kept_out(c // join).start()

        return carry

    lax.fori_loop(0, chunks, chunk, 0)

    dgot[me] = dsum[...]
    for k in range(1, n):
        summed(k).wait()
    lane = lax.broadcasted_iota(jnp.int32, (chans, chans), 1)
    row = lax.broadcasted_iota(jnp.int32, (chans, chans), 0)
    gain = jnp.sum(jnp.where(lane == row, jnp.broadcast_to(skip[...], (chans, chans)), 0.0), axis=1, keepdims=True)
    for t in range(n):
        sums[t:t + 1, :] = dgot[t]
    found = sums[...]
    lane = lax.broadcasted_iota(jnp.int32, (n, chans), 1)
    row = lax.broadcasted_iota(jnp.int32, (n, chans), 0)
    line = jnp.zeros((n, chans), F32)
    for j in range(chunks * per):
        line = jnp.where(lane == j * n + row, found[:, j:j + 1], line)
    o_skip[...] = jnp.sum(line, axis=0, keepdims=True) * scale

    for c in range(chunks):
        down = slice(group * c, group * (c + 1))
        col = jnp.broadcast_to(gain[down], (group, LANES))
        if c % join == 0:
            for k in range(1, n):
                outward(c // join, k).wait()
            kept_out(c // join).wait()
        for q in range(blocks):
            at = (down, slice(LANES * q, LANES * (q + 1)))
            got = []
            for f in range(3):
                got.append(jnp.concatenate([gbuf[c // join, spread(f, i, q, c % join, join), :] for i in range(per)], axis=0))
            post_f, pre_f = post[at].astype(F32), pre[at].astype(F32)
            sig_f, cot_f = sig[at].astype(F32), cot[at].astype(F32)
            conved = got[0] + col * (pre_f * sig_f)
            o_out[at] = (post_f * conved).astype(BF16)
            o_post[at] = (cot_f * conved).astype(BF16)
            d_gated = got[1] + col * (cot_f * post_f)
            o_pre[at] = (d_gated * sig_f).astype(BF16)
            o_sig[at] = (d_gated * pre_f).astype(BF16)
            o_taps[at] = got[2] * scale


def store(*refs):
    half = len(refs) // 2
    for copy in fill(list(zip(refs[:half], refs[half:-1])), refs[-1]):
        copy.wait()


def solution(mesh):
    n = mesh.shape["seq"]
    chunks = 4
    join = 1

    def shards(post_gate, pre_gate, signal, cotangent, filter_taps, skip_gain):
        chans, length = filter_taps.shape
        blocks = length // LANES
        own = chans // n
        per = own // chunks
        first, mid, last, turn = tables(n * blocks, 2 * n * length)
        vmem = pl.BlockSpec(memory_space=pltpu.VMEM)
        hbm = pl.BlockSpec(memory_space=pltpu.HBM)
        half = jax.ShapeDtypeStruct((chans, length), BF16)
        results = (half, half, half, half, jax.ShapeDtypeStruct((1, chans), F32), jax.ShapeDtypeStruct((chans, length), F32))
        gates = pltpu.VMEM((chans, length), BF16)
        wide = pltpu.VMEM((chunks // join, n * 3 * per * blocks * join, LANES), F32)
        both = pltpu.VMEM((chunks // join, n, 3 * per * blocks * join, LANES), F32)
        few = pltpu.SemaphoreType.DMA((chunks // join, n))
        flat = pltpu.VMEM((chunks, n * 3 * per * blocks, LANES), F32)
        cut = pltpu.VMEM((chunks, n, 3 * per * blocks, LANES), F32)
        sem = pltpu.SemaphoreType.DMA((chunks, n))
        operands = (post_gate, pre_gate, signal, cotangent, filter_taps, first, mid, last, turn, skip_gain.reshape(1, chans))
        got = pl.pallas_call(
            functools.partial(exchange, n, chunks, join),
            out_shape=results,
            in_specs=[hbm] * 10,
            out_specs=[vmem] * 6,
            scratch_shapes=[
                gates, gates, gates, gates, pltpu.VMEM((chans, length), F32),
                pltpu.VMEM(first.shape, BF16), pltpu.VMEM(mid.shape, BF16), pltpu.VMEM(last.shape, BF16), pltpu.VMEM(turn.shape, F32),
                pltpu.VMEM((1, chans), F32),
                flat, cut, both, wide,
                pltpu.VMEM((1, LANES), F32), pltpu.VMEM((n, 1, LANES), F32), pltpu.VMEM((n, LANES), F32),
                pltpu.SemaphoreType.DMA((10,)),
                pltpu.SemaphoreType.DMA((2, chunks)), sem, sem, few, few,
                pltpu.SemaphoreType.DMA((n,)), pltpu.SemaphoreType.DMA((n,)),
            ],
            compiler_params=pltpu.CompilerParams(collective_id=0, has_side_effects=True, vmem_limit_bytes=32 << 20),
        )(*[pltpu.with_memory_space_constraint(x, pltpu.HBM) for x in operands])
        outs = pl.pallas_call(
            store,
            out_shape=results,
            in_specs=[vmem] * 6,
            out_specs=[hbm] * 6,
            scratch_shapes=[pltpu.SemaphoreType.DMA((6,))],
            compiler_params=pltpu.CompilerParams(vmem_limit_bytes=32 << 20),
        )(*got)
        return outs[0], outs[1], outs[2], outs[3], outs[4].reshape(chans), outs[5]

    return jax.shard_map(
        shards,
        mesh=mesh,
        in_specs=(P("chan", "seq"),) * 5 + (P("chan"),),
        out_specs=(P("chan", "seq"),) * 4 + (P("chan"), P("chan", "seq")),
        check_vma=False,
    )
```
